32 devices in a mesh: rep: 4 (over y, x), shard: 8 (over z, core).
Axes of the slice: x: 2, y: 2, z: 4, core: 2. Of those that a mesh axis runs over, the one named last changes fastest.
Arguments:
- tokens: bfloat16 [4096, 768], P(('rep', 'shard')), may hold values from -6 to 6
- segment_ids: int32 [32, 128], P(('rep', 'shard')), may hold values from 0 to 3, never falling along the last dimension, each value on 1 to 64 neighbouring positions
- first_gain: bfloat16 [768], P('shard'), may hold values from 0.5 to 1.5
- first_shift: bfloat16 [768], P('shard'), may hold values from -3 to 3
- qkv_weight: bfloat16 [768, 2304], P('shard'), may hold values from -3 to 3, as said below
- qv_bias: bfloat16 [2, 768], P(None, 'shard'), may hold values from -3 to 3
- proj_weight: bfloat16 [768, 768], P('shard'), may hold values from -0.625 to 0.625
- proj_bias: bfloat16 [768], P('shard'), may hold values from -3 to 3
- second_gain: bfloat16 [768], P('shard'), may hold values from 0.5 to 1.5
- second_shift: bfloat16 [768], P('shard'), may hold values from -3 to 3
- fc_weight: bfloat16 [768, 3072], P('shard'), may hold values from -0.21875 to 0.21875
- fc_bias: bfloat16 [3072], P('shard'), may hold values from -3 to 3
- out_weight: bfloat16 [3072, 768], P('shard'), may hold values from -0.109375 to 0.109375
- out_bias: bfloat16 [768], P('shard'), may hold values from -3 to 3
- cotangent: bfloat16 [4096, 768], P(('rep', 'shard')), may hold values from -6 to 6
Outputs:
- block_output: bfloat16 [4096, 768], P(('rep', 'shard'))
- grad_tokens: float32 [4096, 768], P(('rep', 'shard'))
- grad_first_gain: float32 [768], P('shard')
- grad_first_shift: float32 [768], P('shard')
- grad_qkv_weight: float32 [768, 2304], P('shard')
- grad_qv_bias: float32 [2, 768], P(None, 'shard')
- grad_proj_weight: float32 [768, 768], P('shard')
- grad_proj_bias: float32 [768], P('shard')
- grad_second_gain: float32 [768], P('shard')
- grad_second_shift: float32 [768], P('shard')
- grad_fc_weight: float32 [768, 3072], P('shard')
- grad_fc_bias: float32 [3072], P('shard')
- grad_out_weight: float32 [3072, 768], P('shard')
- grad_out_bias: float32 [768], P('shard')
The draws below stay inside these ranges and needn't reach their ends.
Inputs may be any that keep to these rules, and one draw needn't show every extreme that they name: `segment_ids`: each row holds 4 runs of equal numbers in rising order, each run 1 to 64 long, one of them exactly 64. `qkv_weight`: columns 0 to 767 project to queries, the next 768 columns to keys, the last 768 columns to values.
All inputs are finite; a program needn't handle non-finite values.
Results may differ from the reference program's by a relative error of at most 0.011.
Values may be sent and summed in bfloat16 or wider, within the bound.
A program may use at most 128 MiB of HBM per device.

```python
import math
import jax
import jax.numpy as jnp
import numpy as np
from jax import lax

D = 768
HEADS = 12
HD = 64
FF = 3072
TOK_DEV = 128
SEQ_DEV = 4
MOST = 64
TOKENS = 4096
DEVICES = 32


def draw_tokens(key, part):
    fresh_key = jax.random.fold_in(jax.random.fold_in(key, 5), 0)
    drawn_rows = jax.random.normal(fresh_key, (TOKENS, D), jnp.float32)
    return jnp.clip(drawn_rows, -6.0, 6.0).astype(jnp.bfloat16)


def draw_qkv_weight(key, part):
    base_key = jax.random.fold_in(key, 3)
    matrix = jax.random.normal(base_key, (D, 3 * D), jnp.float32) * (1.0 / math.sqrt(D))
    return jnp.clip(matrix, -3.0, 3.0).astype(jnp.bfloat16)


def strengthened(values, own_key, source, target, parts, factor):
    owner, partner = [(jnp.arange(values.shape[axis_at]) // (values.shape[axis_at] // parts)).reshape([-1 if axis == axis_at else 1 for axis in range(values.ndim)]) for axis_at in (source, target)]
    chosen = jax.random.permutation(own_key, parts)[partner]
    strong = (owner == chosen) | (owner == (partner + parts // 2) % parts)
    return jnp.where(strong, factor * values, values)


def level_of(stream_key, extent, cuts, least, high):
    def one(dim, parts):
        heights = jax.random.uniform(jax.random.fold_in(jax.random.fold_in(stream_key, 6), dim), (parts,), jnp.float32, least / len(cuts), high / len(cuts))
        return jnp.repeat(jnp.exp(heights), extent[dim] // parts).reshape((-1,) + (1,) * (len(extent) - dim - 1))

    loudness = one(*cuts[0])
    for cut in cuts[1:]:
        loudness = loudness * one(*cut)
    return loudness


def length_profile(count, total, limit, skew):
    portions = [(1 << 20) // math.isqrt(rank ** skew) + 1 for rank in range(2, count + 1)]
    rest, holding = total - limit - (count - 1), [1] * (count - 1)
    while rest > 0:
        movable = [i for i in range(count - 1) if holding[i] < limit]
        mass, remaining = sum([portions[i] for i in movable]), rest
        for i in movable:
            more = min(limit - holding[i], max(1, remaining * portions[i] // mass), rest)
            holding[i] = holding[i] + more
            rest = rest - more
    return np.array([limit] + holding)


def ragged(own_key, number_of, total, most, slope):
    if number_of == 2:
        one = jax.random.randint(own_key, (), max(1, total - most), min(most, total - 1) + 1)
        return jnp.stack([one, total - one])
    sizes = jnp.asarray(length_profile(number_of, total, most, slope), jnp.int32)
    couples = (number_of - 1) // 2
    donor, taker = sizes[1:1 + 2 * couples:2], sizes[2:2 + 2 * couples:2]
    slack = jnp.minimum(donor - 1, most - taker)
    shifted = jax.random.randint(jax.random.fold_in(own_key, 1), (couples,), 0, 1 << 20) % (slack + 1)
    sizes = sizes.at[1:1 + 2 * couples:2].set(donor - shifted).at[2:2 + 2 * couples:2].set(taker + shifted)
    return sizes[jax.random.permutation(jax.random.fold_in(own_key, 2), number_of)]


def gaussian(own_key, dims, deviation, most, cuts=(), kind=jnp.bfloat16):
    values = jax.random.normal(own_key, dims, jnp.float32) * deviation
    if len(cuts) > 0:
        values = level_of(own_key, dims, cuts, -0.22, 0.18) * values
    return jnp.clip(values, min=-most, max=most).astype(kind)


def heavy_noise(stream_key, dims, scale, most, cuts, heavy, kind=jnp.bfloat16):
    drawn = scale * jax.random.normal(stream_key, dims, jnp.float32)
    if cuts:
        drawn = drawn * level_of(stream_key, dims, cuts, -0.22, 0.18)
    return jnp.clip(strengthened(drawn, jax.random.fold_in(stream_key, 3), *heavy), -most, most).astype(kind)


def setup_inputs(seed: int = 0) -> dict:
    key_list = jax.random.split(jax.random.key(seed), 16)
    tokens = draw_tokens(jax.random.fold_in(key_list[15], 71), 0)
    segment_ids = jax.vmap(lambda own: jnp.searchsorted(jnp.cumsum(ragged(own, SEQ_DEV, TOK_DEV, MOST, 2)), jnp.arange(TOK_DEV), side="right"))(jax.random.split(key_list[1], DEVICES)).reshape((DEVICES, TOK_DEV)).astype(jnp.int32)
    first_gain = jnp.clip(1.0 + 0.1 * jax.random.normal(key_list[2], (D,), jnp.float32), 0.5, 1.5).astype(jnp.bfloat16)
    first_shift = gaussian(key_list[3], (D,), 0.5, 3.0, ((0, 8),))
    qkv_weight = draw_qkv_weight(jax.random.fold_in(key_list[15], 71), 0)
    qv_bias = gaussian(key_list[5], (2, D), 0.5, 3.0, ((1, 8),))
    proj_weight = gaussian(key_list[6], (D, D), (D // 8) ** -0.5, 0.625, ((0, 8),))
    proj_bias = gaussian(key_list[7], (D,), 0.5, 3.0, ((0, 8),))
    second_gain = jnp.clip(1.0 + 0.1 * jax.random.normal(key_list[8], (D,), jnp.float32), 0.5, 1.5).astype(jnp.bfloat16)
    second_shift = gaussian(key_list[9], (D,), 0.5, 3.0, ((0, 8),))
    fc_weight = gaussian(key_list[10], (D, FF), D ** -0.5, 0.21875, ((0, 8),))
    fc_bias = gaussian(key_list[11], (FF,), 0.5, 3.0, ((0, 8),))
    out_weight = gaussian(key_list[12], (FF, D), FF ** -0.5, 0.109375, ((0, 8),))
    out_bias = gaussian(key_list[13], (D,), 0.5, 3.0, ((0, 8),))
    cotangent = heavy_noise(key_list[14], (TOKENS, D), 1.0, 6.0, ((0, 32),), (0, 1, 32, 2.75))
    return {"tokens": tokens, "segment_ids": segment_ids, "first_gain": first_gain, "first_shift": first_shift, "qkv_weight": qkv_weight, "qv_bias": qv_bias, "proj_weight": proj_weight, "proj_bias": proj_bias, "second_gain": second_gain, "second_shift": second_shift, "fc_weight": fc_weight, "fc_bias": fc_bias, "out_weight": out_weight, "out_bias": out_bias, "cotangent": cotangent}


EPSILON = 1e-05

def layer_norm(field, norm_gain, norm_shift):
    center = field - lax.optimization_barrier(jnp.mean(field, axis=-1, keepdims=True))
    spread = lax.optimization_barrier(jnp.mean(center * center, axis=-1, keepdims=True))
    return center * lax.rsqrt(spread + EPSILON) * norm_gain + norm_shift

def gelu_tanh(field):
    return jax.nn.gelu(field, approximate=True)

def head_split(matrix):
    return matrix.reshape(matrix.shape[0], HEADS, HD).astype(jnp.float32)

def masked_scores(query, keys, segments):
    rows = query.shape[0]
    scores = jnp.einsum('qhd,khd->hqk', head_split(query), head_split(keys)) * (1.0 / math.sqrt(HD))
    position = jnp.arange(rows, dtype=jnp.int32)
    allowed = (segments[:, None] == segments[None, :]) & (position[None, :] <= position[:, None])
    return jnp.where(allowed[None], scores, -1e+30)

def attend_forward(query, keys, values, segments):
    rows = query.shape[0]
    scores = masked_scores(query, keys, segments)
    row_max = lax.optimization_barrier(jnp.max(scores, axis=-1, keepdims=True))
    row_total = lax.optimization_barrier(jnp.sum(jnp.exp(scores - row_max), axis=-1, keepdims=True))
    logsum = row_max + jnp.log(row_total)
    probs = jnp.exp(scores - logsum).astype(jnp.bfloat16)
    attended = jnp.einsum('hqk,khd->qhd', probs.astype(jnp.float32), head_split(values))
    return (attended.reshape(rows, D).astype(jnp.bfloat16), logsum)

def attend_backward(query, keys, values, segments, attended, logsum, grad_attended):
    rows = query.shape[0]
    scores = masked_scores(query, keys, segments)
    weights = jnp.exp(scores - logsum)
    probs_low = weights.astype(jnp.bfloat16).astype(jnp.float32)
    grad_heads = head_split(grad_attended)
    grad_values = jnp.einsum('hqk,qhd->khd', probs_low, grad_heads)
    grad_probs = jnp.einsum('qhd,khd->hqk', grad_heads, head_split(values))
    delta = jnp.einsum('qhd,qhd->hq', grad_heads, head_split(attended))[..., None]
    grad_scores = (weights * (grad_probs - delta) * (1.0 / math.sqrt(HD))).astype(jnp.bfloat16).astype(jnp.float32)
    grad_query = jnp.einsum('hqk,khd->qhd', grad_scores, head_split(keys))
    grad_keys = jnp.einsum('hqk,qhd->khd', grad_scores, head_split(query))
    return (grad_query.reshape(rows, D), grad_keys.reshape(rows, D), grad_values.reshape(rows, D))

def block_pass(tok_block, cot_block, segments, weights):
    first_gain, first_shift, qkv_weight, qv_bias, proj_weight, proj_bias, second_gain, second_shift, fc_weight, fc_bias, out_weight, out_bias = weights
    inputs = tok_block.astype(jnp.float32)
    normed_f, first_back = jax.vjp(layer_norm, inputs, first_gain.astype(jnp.float32), first_shift.astype(jnp.float32))
    normed_first = normed_f.astype(jnp.bfloat16)
    projected = jnp.dot(normed_first, qkv_weight, preferred_element_type=jnp.float32)
    query = (projected[:, :D] + qv_bias[0].astype(jnp.float32)).astype(jnp.bfloat16)
    keys = projected[:, D:2 * D].astype(jnp.bfloat16)
    values = (projected[:, 2 * D:] + qv_bias[1].astype(jnp.float32)).astype(jnp.bfloat16)
    attended, logsum = attend_forward(query, keys, values, segments)
    residual = inputs + jnp.dot(attended, proj_weight, preferred_element_type=jnp.float32) + proj_bias.astype(jnp.float32)
    normed_s, second_back = jax.vjp(layer_norm, residual, second_gain.astype(jnp.float32), second_shift.astype(jnp.float32))
    normed_second = normed_s.astype(jnp.bfloat16)
    pre_act = jnp.dot(normed_second, fc_weight, preferred_element_type=jnp.float32) + fc_bias.astype(jnp.float32)
    activated, gelu_back = jax.vjp(gelu_tanh, pre_act)
    hidden = activated.astype(jnp.bfloat16)
    result = (residual + jnp.dot(hidden, out_weight, preferred_element_type=jnp.float32) + out_bias.astype(jnp.float32)).astype(jnp.bfloat16)
    cot_f = cot_block.astype(jnp.float32)
    term_out_bias = lax.optimization_barrier(jnp.sum(cot_f, axis=0))
    term_out_weight = jnp.dot(hidden.T, cot_block, preferred_element_type=jnp.float32)
    grad_hidden = jnp.dot(cot_block, out_weight.T, preferred_element_type=jnp.float32)
    grad_pre, = gelu_back(grad_hidden)
    grad_pre_low = grad_pre.astype(jnp.bfloat16)
    term_fc_bias = lax.optimization_barrier(jnp.sum(grad_pre, axis=0))
    term_fc_weight = jnp.dot(normed_second.T, grad_pre_low, preferred_element_type=jnp.float32)
    grad_normed_second = jnp.dot(grad_pre_low, fc_weight.T, preferred_element_type=jnp.float32)
    grad_from_norm, term_second_gain, term_second_shift = second_back(grad_normed_second)
    grad_residual = cot_f + grad_from_norm
    grad_residual_low = grad_residual.astype(jnp.bfloat16)
    term_proj_bias = lax.optimization_barrier(jnp.sum(grad_residual, axis=0))
    term_proj_weight = jnp.dot(attended.T, grad_residual_low, preferred_element_type=jnp.float32)
    grad_attended = jnp.dot(grad_residual_low, proj_weight.T, preferred_element_type=jnp.float32).astype(jnp.bfloat16)
    grad_query, grad_keys, grad_values = attend_backward(query, keys, values, segments, attended, logsum, grad_attended)
    term_qv_bias = jnp.stack([lax.optimization_barrier(jnp.sum(grad_query, axis=0)), lax.optimization_barrier(jnp.sum(grad_values, axis=0))])
    grad_projected = jnp.concatenate([grad_query, grad_keys, grad_values], axis=1).astype(jnp.bfloat16)
    term_qkv_weight = jnp.dot(normed_first.T, grad_projected, preferred_element_type=jnp.float32)
    grad_normed_first = jnp.dot(grad_projected, qkv_weight.T, preferred_element_type=jnp.float32)
    grad_input_norm, term_first_gain, term_first_shift = first_back(grad_normed_first)
    grad_inputs = grad_residual + grad_input_norm
    terms = (term_first_gain, term_first_shift, term_qkv_weight, term_qv_bias, term_proj_weight, term_proj_bias, term_second_gain, term_second_shift, term_fc_weight, term_fc_bias, term_out_weight, term_out_bias)
    return (result, grad_inputs, terms)

def reference(tokens, segment_ids, first_gain, first_shift, qkv_weight, qv_bias, proj_weight, proj_bias, second_gain, second_shift, fc_weight, fc_bias, out_weight, out_bias, cotangent):
    weights = (first_gain, first_shift, qkv_weight, qv_bias, proj_weight, proj_bias, second_gain, second_shift, fc_weight, fc_bias, out_weight, out_bias)
    token_blocks = tokens.reshape(DEVICES, TOK_DEV, D)
    cot_blocks = cotangent.reshape(DEVICES, TOK_DEV, D)
    initial = tuple((jnp.zeros(weight.shape, jnp.float32) for weight in weights))

    def advance(running, pieces):
        tok_block, cot_block, seg_row = pieces
        result, grad_inputs, terms = block_pass(tok_block, cot_block, seg_row, weights)
        return (tuple((total + term for total, term in zip(running, terms))), (result, grad_inputs))
    totals, (results, grad_all) = lax.scan(advance, initial, (token_blocks, cot_blocks, segment_ids))
    factor = 1.0 / math.sqrt(TOKENS)
    return (results.reshape(TOKENS, D), grad_all.reshape(TOKENS, D), totals[0] * factor, totals[1] * factor, totals[2] * factor, totals[3] * factor, totals[4] * factor, totals[5] * factor, totals[6] * factor, totals[7] * factor, totals[8] * factor, totals[9] * factor, totals[10] * factor, totals[11] * factor)
```

```python
import math

import jax
import jax.numpy as jnp
from jax import lax
from jax.sharding import PartitionSpec as P

D = 768
HEADS = 12
HD = 64


EPSILON = 1e-05


def layer_norm(field, norm_gain, norm_shift):
    center = field - jnp.mean(field, axis=-1, keepdims=True)
    spread = jnp.mean(center * center, axis=-1, keepdims=True)
    return center * lax.rsqrt(spread + EPSILON) * norm_gain + norm_shift


def gelu_tanh(field):
    return jax.nn.gelu(field, approximate=True)


def head_split(matrix):
    return matrix.reshape(matrix.shape[0], HEADS, HD)


def masked_scores(query, keys, segments):
    rows = query.shape[0]
    scores = jnp.einsum(
        "qhd,khd->hqk", head_split(query), head_split(keys), preferred_element_type=jnp.float32
    ) * (1.0 / math.sqrt(HD))
    position = lax.iota(jnp.int32, rows)
    allowed = (segments[:, None] == segments[None, :]) & (position[None, :] <= position[:, None])
    return jnp.where(allowed[None], scores, -1e30)


def attend_forward(query, keys, values, segments):
    rows = query.shape[0]
    scores = masked_scores(query, keys, segments)
    row_max = jnp.max(scores, axis=-1, keepdims=True)
    row_total = jnp.sum(jnp.exp(scores - row_max), axis=-1, keepdims=True)
    logsum = row_max + jnp.log(row_total)
    probs = jnp.exp(scores - logsum).astype(jnp.bfloat16)
    attended = jnp.einsum(
        "hqk,khd->qhd", probs, head_split(values), preferred_element_type=jnp.float32
    )
    return (attended.reshape(rows, D).astype(jnp.bfloat16), logsum)


def attend_backward(query, keys, values, segments, attended, logsum, grad_attended):
    rows = query.shape[0]
    scores = masked_scores(query, keys, segments)
    weights = jnp.exp(scores - logsum)
    grad_heads = head_split(grad_attended)
    grad_values = jnp.einsum(
        "hqk,qhd->khd", weights.astype(jnp.bfloat16), grad_heads, preferred_element_type=jnp.float32
    )
    grad_probs = jnp.einsum(
        "qhd,khd->hqk", grad_heads, head_split(values), preferred_element_type=jnp.float32
    )
    delta = jnp.einsum(
        "qhd,qhd->hq", grad_heads, head_split(attended), preferred_element_type=jnp.float32
    )
    grad_scores = (weights * (grad_probs - delta[..., None]) * (1.0 / math.sqrt(HD))).astype(
        jnp.bfloat16
    )
    grad_query = jnp.einsum(
        "hqk,khd->qhd", grad_scores, head_split(keys), preferred_element_type=jnp.float32
    )
    grad_keys = jnp.einsum(
        "hqk,qhd->khd", grad_scores, head_split(query), preferred_element_type=jnp.float32
    )
    return (grad_query.reshape(rows, D), grad_keys.reshape(rows, D), grad_values.reshape(rows, D))


def per_device(
    tokens,
    segment_ids,
    first_gain,
    first_shift,
    qkv_weight,
    qv_bias,
    proj_weight,
    proj_bias,
    second_gain,
    second_shift,
    fc_weight,
    fc_bias,
    out_weight,
    out_bias,
    cotangent,
):
    low = jnp.bfloat16
    segments = segment_ids[0]
    own_rows = tokens.shape[0]
    shards = lax.axis_size("shard")
    reps = lax.axis_size("rep")
    factor = 1.0 / math.sqrt(own_rows * reps * shards)
    small = jnp.stack(
        [first_gain, first_shift, qv_bias[0], qv_bias[1], proj_bias, second_gain, second_shift, out_bias]
    )
    small_full = lax.all_gather(small, "shard", axis=1, tiled=True).astype(jnp.float32)
    gain_one, shift_one, q_bias, v_bias, proj_bias_full, gain_two, shift_two, out_bias_full = (
        small_full[i] for i in range(8)
    )
    qkv_full = lax.all_gather(qkv_weight, "shard", axis=0, tiled=True)
    proj_full = lax.all_gather(proj_weight, "shard", axis=0, tiled=True)
    fc_cols = lax.all_to_all(fc_weight, "shard", split_axis=1, concat_axis=0, tiled=True)
    cot_all = lax.all_gather(cotangent, "shard", axis=0, tiled=True)

    inputs = tokens.astype(jnp.float32)
    normed_f, first_back = jax.vjp(layer_norm, inputs, gain_one, shift_one)
    normed_first = normed_f.astype(low)
    projected = jnp.dot(normed_first, qkv_full, preferred_element_type=jnp.float32)
    query = (projected[:, :D] + q_bias).astype(low)
    keys = projected[:, D : 2 * D].astype(low)
    values = (projected[:, 2 * D :] + v_bias).astype(low)
    attended, logsum = attend_forward(query, keys, values, segments)
    residual = (
        inputs + jnp.dot(attended, proj_full, preferred_element_type=jnp.float32) + proj_bias_full
    )
    cot_f = cotangent.astype(jnp.float32)
    term_out_bias = jnp.sum(cot_f, axis=0) * factor
    normed_s, second_back = jax.vjp(layer_norm, residual, gain_two, shift_two)
    normed_second = normed_s.astype(low)
    normed_all = lax.all_gather(normed_second, "shard", axis=0, tiled=True)
    pre_act = jnp.dot(normed_all, fc_cols, preferred_element_type=jnp.float32) + fc_bias.astype(
        jnp.float32
    )
    activated, gelu_back = jax.vjp(gelu_tanh, pre_act)
    hidden = activated.astype(low)
    grad_hidden = jnp.dot(cot_all, out_weight.T, preferred_element_type=jnp.float32)
    (grad_pre,) = gelu_back(grad_hidden)
    grad_pre_low = grad_pre.astype(low)
    term_fc_bias = jnp.sum(grad_pre, axis=0) * factor
    grad_normed_part = jnp.dot(grad_pre_low, fc_cols.T, preferred_element_type=jnp.float32).astype(low)
    grad_normed_second = lax.psum_scatter(
        grad_normed_part, "shard", scatter_dimension=0, tiled=True
    ).astype(jnp.float32)
    out_part = jnp.dot(hidden, out_weight, preferred_element_type=jnp.float32).astype(low)
    out_sum = lax.psum_scatter(out_part, "shard", scatter_dimension=0, tiled=True).astype(jnp.float32)
    result = (residual + out_sum + out_bias_full).astype(low)
    term_out_weight = (
        jnp.dot(hidden.T, cot_all, preferred_element_type=jnp.float32) * factor
    ).astype(low)
    term_fc_weight = (
        jnp.dot(normed_all.T, grad_pre_low, preferred_element_type=jnp.float32) * factor
    ).astype(low)
    out_piece = lax.psum_scatter(term_out_weight, "rep", scatter_dimension=0, tiled=True)
    out_grad = lax.all_gather(out_piece, "rep", axis=0, tiled=True).astype(jnp.float32)
    fc_own = D // (shards * reps)
    fc_rows = term_fc_weight.reshape(shards, reps, fc_own, -1).swapaxes(0, 1).reshape(D, -1)
    fc_piece = lax.psum_scatter(fc_rows, "rep", scatter_dimension=0, tiled=True)
    fc_piece = lax.all_to_all(fc_piece, "shard", split_axis=0, concat_axis=1, tiled=True)
    fc_grad = lax.all_gather(fc_piece, "rep", axis=0, tiled=True).astype(jnp.float32)

    grad_from_norm, second_gain_sum, second_shift_sum = second_back(grad_normed_second)
    grad_residual = cot_f + grad_from_norm
    grad_residual_low = grad_residual.astype(low)
    term_proj_bias = jnp.sum(grad_residual, axis=0) * factor
    term_proj_weight = (
        jnp.dot(attended.T, grad_residual_low, preferred_element_type=jnp.float32) * factor
    ).astype(low)
    grad_attended = jnp.dot(
        grad_residual_low, proj_full.T, preferred_element_type=jnp.float32
    ).astype(low)
    grad_query, grad_keys, grad_values = attend_backward(
        query, keys, values, segments, attended, logsum, grad_attended
    )
    grad_projected = jnp.concatenate([grad_query, grad_keys, grad_values], axis=1).astype(low)
    term_qkv_weight = (
        jnp.dot(normed_first.T, grad_projected, preferred_element_type=jnp.float32) * factor
    ).astype(low)
    grad_normed_first = jnp.dot(grad_projected, qkv_full.T, preferred_element_type=jnp.float32)
    grad_input_norm, first_gain_sum, first_shift_sum = first_back(grad_normed_first)
    grad_inputs = grad_residual + grad_input_norm

    proj_share = lax.psum_scatter(term_proj_weight, "shard", scatter_dimension=0, tiled=True)
    qkv_share = lax.psum_scatter(term_qkv_weight, "shard", scatter_dimension=0, tiled=True)
    proj_piece = lax.psum_scatter(proj_share, "rep", scatter_dimension=0, tiled=True)
    qkv_piece = lax.psum_scatter(qkv_share, "rep", scatter_dimension=0, tiled=True)
    proj_grad = lax.all_gather(proj_piece, "rep", axis=0, tiled=True).astype(jnp.float32)
    qkv_grad = lax.all_gather(qkv_piece, "rep", axis=0, tiled=True).astype(jnp.float32)
    terms = jnp.stack(
        [
            first_gain_sum * factor,
            first_shift_sum * factor,
            jnp.sum(grad_query, axis=0) * factor,
            jnp.sum(grad_values, axis=0) * factor,
            term_proj_bias,
            second_gain_sum * factor,
            second_shift_sum * factor,
            term_out_bias,
        ]
    )
    sums, fc_bias_grad = lax.psum(
        (lax.psum_scatter(terms, "shard", scatter_dimension=1, tiled=True), term_fc_bias), "rep"
    )
    return (
        result,
        grad_inputs,
        sums[0],
        sums[1],
        qkv_grad,
        sums[2:4],
        proj_grad,
        sums[4],
        sums[5],
        sums[6],
        fc_grad,
        fc_bias_grad,
        out_grad,
        sums[7],
    )


def solution(mesh):
    return jax.shard_map(
        per_device,
        mesh=mesh,
        in_specs=(
            P(("rep", "shard"), None),
            P(("rep", "shard"), None),
            P("shard"),
            P("shard"),
            P("shard", None),
            P(None, "shard"),
            P("shard", None),
            P("shard"),
            P("shard"),
            P("shard"),
            P("shard", None),
            P("shard"),
            P("shard", None),
            P("shard"),
            P(("rep", "shard"), None),
        ),
        out_specs=(
            P(("rep", "shard"), None),
            P(("rep", "shard"), None),
            P("shard"),
            P("shard"),
            P("shard", None),
            P(None, "shard"),
            P("shard", None),
            P("shard"),
            P("shard"),
            P("shard"),
            P("shard", None),
            P("shard"),
            P("shard", None),
            P("shard"),
        ),
        check_vma=False,
    )
```

```python
import math

import jax
import jax.numpy as jnp
from jax import lax
from jax.sharding import PartitionSpec as P

D = 768
HEADS = 12
HD = 64
FF = 3072


EPSILON = 1e-05


def layer_norm(field, norm_gain, norm_shift):
    center = field - jnp.mean(field, axis=-1, keepdims=True)
    spread = jnp.mean(center * center, axis=-1, keepdims=True)
    return center * lax.rsqrt(spread + EPSILON) * norm_gain + norm_shift


def gelu_tanh(field):
    return jax.nn.gelu(field, approximate=True)


def head_split(matrix):
    return matrix.reshape(matrix.shape[0], HEADS, HD)


def masked_scores(query, keys, segments):
    rows = query.shape[0]
    scores = jnp.einsum(
        "qhd,khd->hqk", head_split(query), head_split(keys), preferred_element_type=jnp.float32
    ) * (1.0 / math.sqrt(HD))
    position = lax.iota(jnp.int32, rows)
    allowed = (segments[:, None] == segments[None, :]) & (position[None, :] <= position[:, None])
    return jnp.where(allowed[None], scores, -1e30)


def attend_forward(query, keys, values, segments):
    rows = query.shape[0]
    scores = masked_scores(query, keys, segments)
    row_max = jnp.max(scores, axis=-1, keepdims=True)
    row_total = jnp.sum(jnp.exp(scores - row_max), axis=-1, keepdims=True)
    logsum = row_max + jnp.log(row_total)
    probs = jnp.exp(scores - logsum).astype(jnp.bfloat16)
    attended = jnp.einsum(
        "hqk,khd->qhd", probs, head_split(values), preferred_element_type=jnp.float32
    )
    return (attended.reshape(rows, D).astype(jnp.bfloat16), logsum)


def attend_backward(query, keys, values, segments, attended, logsum, grad_attended):
    rows = query.shape[0]
    scores = masked_scores(query, keys, segments)
    weights = jnp.exp(scores - logsum)
    grad_heads = head_split(grad_attended)
    grad_values = jnp.einsum(
        "hqk,qhd->khd", weights.astype(jnp.bfloat16), grad_heads, preferred_element_type=jnp.float32
    )
    grad_probs = jnp.einsum(
        "qhd,khd->hqk", grad_heads, head_split(values), preferred_element_type=jnp.float32
    )
    delta = jnp.einsum(
        "qhd,qhd->hq", grad_heads, head_split(attended), preferred_element_type=jnp.float32
    )
    grad_scores = (weights * (grad_probs - delta[..., None]) * (1.0 / math.sqrt(HD))).astype(
        jnp.bfloat16
    )
    grad_query = jnp.einsum(
        "hqk,khd->qhd", grad_scores, head_split(keys), preferred_element_type=jnp.float32
    )
    grad_keys = jnp.einsum(
        "hqk,qhd->khd", grad_scores, head_split(query), preferred_element_type=jnp.float32
    )
    return (grad_query.reshape(rows, D), grad_keys.reshape(rows, D), grad_values.reshape(rows, D))


def exchange(field, axis, split, concat):
    return lax.all_to_all(field, axis, split_axis=split, concat_axis=concat, tiled=True)


def sum_exchanged(field, axis):
    parts = lax.axis_size(axis)
    blocks = exchange(field.reshape((parts, -1) + field.shape[1:]), axis, 0, 0)
    return jnp.sum(blocks.astype(jnp.float32), axis=0)


def spread(field, axis):
    parts = lax.axis_size(axis)
    return exchange(jnp.broadcast_to(field[None], (parts,) + field.shape), axis, 0, 0)


def by_replica(field, shards, reps):
    rows = field.shape[0]
    return (
        field.reshape(shards, reps, rows // (shards * reps), -1).swapaxes(0, 1).reshape(rows, -1)
    )


def per_device(
    tokens,
    segment_ids,
    first_gain,
    first_shift,
    qkv_weight,
    qv_bias,
    proj_weight,
    proj_bias,
    second_gain,
    second_shift,
    fc_weight,
    fc_bias,
    out_weight,
    out_bias,
    cotangent,
):
    low = jnp.bfloat16
    segments = segment_ids[0]
    own_rows = tokens.shape[0]
    shards = lax.axis_size("shard")
    reps = lax.axis_size("rep")
    factor = 1.0 / math.sqrt(own_rows * reps * shards)
    small = jnp.stack(
        [first_gain, first_shift, qv_bias[0], qv_bias[1], proj_bias, second_gain, second_shift, out_bias]
    )
    small_full = lax.all_gather(small, "shard", axis=1, tiled=True).astype(jnp.float32)
    gain_one, shift_one, q_bias, v_bias, proj_bias_full, gain_two, shift_two, out_bias_full = (
        small_full[i] for i in range(8)
    )
    proj_full = lax.all_gather(proj_weight, "shard", axis=0, tiled=True)
    qkv_cols = exchange(qkv_weight, "shard", 1, 0)
    fc_cols = exchange(fc_weight, "shard", 1, 0)
    qkv_bias = jnp.concatenate([q_bias, jnp.zeros_like(q_bias), v_bias])
    width = qkv_cols.shape[1]
    bias_cols = lax.dynamic_slice_in_dim(qkv_bias, lax.axis_index("shard") * width, width)

    inputs = tokens.astype(jnp.float32)
    normed_f, first_back = jax.vjp(layer_norm, inputs, gain_one, shift_one)
    first_all = lax.all_gather(normed_f.astype(low), "shard", axis=0, tiled=True)
    cot_later, first_all = lax.optimization_barrier((cotangent, first_all))
    cot_all = lax.all_gather(cot_later, "shard", axis=0, tiled=True)
    projected_cols = jnp.dot(first_all, qkv_cols, preferred_element_type=jnp.float32) + bias_cols
    projected = exchange(projected_cols.astype(low), "shard", 0, 1)
    query = projected[:, :D]
    keys = projected[:, D : 2 * D]
    values = projected[:, 2 * D :]
    attended, logsum = attend_forward(query, keys, values, segments)
    residual = (
        inputs + jnp.dot(attended, proj_full, preferred_element_type=jnp.float32) + proj_bias_full
    )
    cot_f = cotangent.astype(jnp.float32)
    normed_s, second_back = jax.vjp(layer_norm, residual, gain_two, shift_two)
    normed_all = lax.all_gather(normed_s.astype(low), "shard", axis=0, tiled=True)
    pre_act = jnp.dot(normed_all, fc_cols, preferred_element_type=jnp.float32) + fc_bias.astype(
        jnp.float32
    )
    activated, gelu_back = jax.vjp(gelu_tanh, pre_act)
    hidden = activated.astype(low)
    grad_hidden = jnp.dot(cot_all, out_weight.T, preferred_element_type=jnp.float32)
    (grad_pre,) = gelu_back(grad_hidden)
    grad_pre_low = grad_pre.astype(low)
    grad_normed_part = jnp.dot(grad_pre_low, fc_cols.T, preferred_element_type=jnp.float32).astype(low)
    grad_normed_low = lax.psum_scatter(grad_normed_part, "shard", scatter_dimension=0, tiled=True)
    term_out_weight = jnp.dot(hidden.T, cot_all, preferred_element_type=jnp.float32) * factor
    term_fc_weight = jnp.dot(normed_all.T, grad_pre_low, preferred_element_type=jnp.float32) * factor
    out_part = jnp.dot(hidden, out_weight, preferred_element_type=jnp.float32).astype(low)
    out_part, attended_later, grad_normed_low = lax.optimization_barrier(
        (out_part, attended, grad_normed_low)
    )
    grad_normed_second = grad_normed_low.astype(jnp.float32)

    grad_from_norm, second_gain_sum, second_shift_sum = second_back(grad_normed_second)
    grad_residual = cot_f + grad_from_norm
    grad_residual_low = grad_residual.astype(low)
    grad_residual_all = lax.all_gather(grad_residual_low, "shard", axis=0, tiled=True)
    attended_cols = exchange(attended_later, "shard", 1, 0)
    grad_attended = jnp.dot(
        grad_residual_low, proj_full.T, preferred_element_type=jnp.float32
    ).astype(low)
    result = (residual + sum_exchanged(out_part, "shard") + out_bias_full).astype(low)
    out_piece = sum_exchanged(term_out_weight.astype(low), "rep").astype(low)
    fc_piece = sum_exchanged(by_replica(term_fc_weight.astype(low), shards, reps), "rep").astype(low)
    fc_piece = exchange(fc_piece, "shard", 0, 1)
    ff_all = spread(jnp.concatenate([out_piece, fc_piece.reshape(-1, D)]), "rep").astype(jnp.float32)
    out_rows = out_piece.shape[0]
    out_grad = ff_all[:, :out_rows].reshape(-1, D)
    fc_grad = ff_all[:, out_rows:].reshape(-1, FF)

    grad_query, grad_keys, grad_values = attend_backward(
        query, keys, values, segments, attended, logsum, grad_attended
    )
    grad_projected = jnp.concatenate([grad_query, grad_keys, grad_values], axis=1).astype(low)
    grad_cols = exchange(grad_projected, "shard", 1, 0)
    grad_first_part = jnp.dot(grad_cols, qkv_cols.T, preferred_element_type=jnp.float32).astype(low)
    grad_normed_first = lax.psum_scatter(
        grad_first_part, "shard", scatter_dimension=0, tiled=True
    ).astype(jnp.float32)
    term_qkv_weight = jnp.dot(first_all.T, grad_cols, preferred_element_type=jnp.float32) * factor
    term_proj_weight = (
        jnp.dot(attended_cols.T, grad_residual_all, preferred_element_type=jnp.float32) * factor
    )
    proj_piece = sum_exchanged(term_proj_weight.astype(low), "rep").astype(low)
    qkv_piece = sum_exchanged(by_replica(term_qkv_weight.astype(low), shards, reps), "rep").astype(low)
    qkv_piece = exchange(qkv_piece, "shard", 0, 1)
    attn_all = spread(jnp.concatenate([proj_piece, qkv_piece.reshape(-1, D)]), "rep").astype(
        jnp.float32
    )
    proj_rows = proj_piece.shape[0]
    proj_grad = attn_all[:, :proj_rows].reshape(-1, D)
    qkv_grad = attn_all[:, proj_rows:].reshape(-1, 3 * D)

    grad_input_norm, first_gain_sum, first_shift_sum = first_back(grad_normed_first)
    grad_inputs = grad_residual + grad_input_norm
    terms = jnp.stack(
        [
            first_gain_sum,
            first_shift_sum,
            jnp.sum(grad_query, axis=0),
            jnp.sum(grad_values, axis=0),
            jnp.sum(grad_residual, axis=0),
            second_gain_sum,
            second_shift_sum,
            jnp.sum(cot_f, axis=0),
        ]
    )
    count = terms.shape[0]
    terms = terms.reshape(count, shards, -1).swapaxes(0, 1).reshape(shards, -1)
    own_terms = jnp.concatenate(
        [jnp.sum(exchange(terms, "shard", 0, 0), axis=0), jnp.sum(grad_pre, axis=0)]
    )
    sums = jnp.sum(spread(own_terms, "rep"), axis=0) * factor
    own_cols = D // shards
    fc_bias_grad = sums[count * own_cols :]
    sums = sums[: count * own_cols].reshape(count, own_cols)
    return (
        result,
        grad_inputs,
        sums[0],
        sums[1],
        qkv_grad,
        sums[2:4],
        proj_grad,
        sums[4],
        sums[5],
        sums[6],
        fc_grad,
        fc_bias_grad,
        out_grad,
        sums[7],
    )


def solution(mesh):
    return jax.shard_map(
        per_device,
        mesh=mesh,
        in_specs=(
            P(("rep", "shard"), None),
            P(("rep", "shard"), None),
            P("shard"),
            P("shard"),
            P("shard", None),
            P(None, "shard"),
            P("shard", None),
            P("shard"),
            P("shard"),
            P("shard"),
            P("shard", None),
            P("shard"),
            P("shard", None),
            P("shard"),
            P(("rep", "shard"), None),
        ),
        out_specs=(
            P(("rep", "shard"), None),
            P(("rep", "shard"), None),
            P("shard"),
            P("shard"),
            P("shard", None),
            P(None, "shard"),
            P("shard", None),
            P("shard"),
            P("shard"),
            P("shard"),
            P("shard", None),
            P("shard"),
            P("shard", None),
            P("shard"),
        ),
        check_vma=False,
    )
```

```python
import math

import jax
import jax.numpy as jnp
from jax import lax
from jax.sharding import PartitionSpec as P

D = 768
HEADS = 12
HD = 64
FF = 3072


EPSILON = 1e-05


def layer_norm(field, norm_gain, norm_shift):
    center = field - jnp.mean(field, axis=-1, keepdims=True)
    spread = jnp.mean(center * center, axis=-1, keepdims=True)
    return center * lax.rsqrt(spread + EPSILON) * norm_gain + norm_shift


def gelu_tanh(field):
    return jax.nn.gelu(field, approximate=True)


def head_split(matrix):
    return matrix.reshape(matrix.shape[0], HEADS, HD)


def masked_scores(query, keys, segments):
    rows = query.shape[0]
    scores = jnp.einsum(
        "qhd,khd->hqk", head_split(query), head_split(keys), preferred_element_type=jnp.float32
    ) * (1.0 / math.sqrt(HD))
    position = lax.iota(jnp.int32, rows)
    allowed = (segments[:, None] == segments[None, :]) & (position[None, :] <= position[:, None])
    return jnp.where(allowed[None], scores, -1e30)


def attend_forward(query, keys, values, segments):
    rows = query.shape[0]
    scores = masked_scores(query, keys, segments)
    row_max = jnp.max(scores, axis=-1, keepdims=True)
    row_total = jnp.sum(jnp.exp(scores - row_max), axis=-1, keepdims=True)
    logsum = row_max + jnp.log(row_total)
    probs = jnp.exp(scores - logsum).astype(jnp.bfloat16)
    attended = jnp.einsum(
        "hqk,khd->qhd", probs, head_split(values), preferred_element_type=jnp.float32
    )
    return (attended.reshape(rows, D).astype(jnp.bfloat16), logsum)


def attend_backward(query, keys, values, segments, attended, logsum, grad_attended):
    rows = query.shape[0]
    scores = masked_scores(query, keys, segments)
    weights = jnp.exp(scores - logsum)
    grad_heads = head_split(grad_attended)
    grad_values = jnp.einsum(
        "hqk,qhd->khd", weights.astype(jnp.bfloat16), grad_heads, preferred_element_type=jnp.float32
    )
    grad_probs = jnp.einsum(
        "qhd,khd->hqk", grad_heads, head_split(values), preferred_element_type=jnp.float32
    )
    delta = jnp.einsum(
        "qhd,qhd->hq", grad_heads, head_split(attended), preferred_element_type=jnp.float32
    )
    grad_scores = (weights * (grad_probs - delta[..., None]) * (1.0 / math.sqrt(HD))).astype(
        jnp.bfloat16
    )
    grad_query = jnp.einsum(
        "hqk,khd->qhd", grad_scores, head_split(keys), preferred_element_type=jnp.float32
    )
    grad_keys = jnp.einsum(
        "hqk,qhd->khd", grad_scores, head_split(query), preferred_element_type=jnp.float32
    )
    return (grad_query.reshape(rows, D), grad_keys.reshape(rows, D), grad_values.reshape(rows, D))


def exchange(field, axis, split, concat):
    return lax.all_to_all(field, axis, split_axis=split, concat_axis=concat, tiled=True)


def spread(field, axis):
    parts = lax.axis_size(axis)
    return exchange(jnp.broadcast_to(field[None], (parts,) + field.shape), axis, 0, 0)


def by_replica(field, shards, reps):
    rows = field.shape[0]
    return (
        field.reshape(shards, reps, rows // (shards * reps), -1).swapaxes(0, 1).reshape(rows, -1)
    )


def per_device(
    tokens,
    segment_ids,
    first_gain,
    first_shift,
    qkv_weight,
    qv_bias,
    proj_weight,
    proj_bias,
    second_gain,
    second_shift,
    fc_weight,
    fc_bias,
    out_weight,
    out_bias,
    cotangent,
):
    low = jnp.bfloat16
    segments = segment_ids[0]
    own_rows = tokens.shape[0]
    shards = lax.axis_size("shard")
    reps = lax.axis_size("rep")
    factor = 1.0 / math.sqrt(own_rows * reps * shards)
    small = jnp.stack(
        [first_gain, first_shift, qv_bias[0], qv_bias[1], proj_bias, second_gain, second_shift, out_bias]
    )
    small_full = lax.all_gather(small, "shard", axis=1, tiled=True).astype(jnp.float32)
    gain_one, shift_one, q_bias, v_bias, proj_bias_full, gain_two, shift_two, out_bias_full = (
        small_full[i] for i in range(8)
    )
    qkv_full = lax.all_gather(qkv_weight, "shard", axis=0, tiled=True)
    proj_full = lax.all_gather(proj_weight, "shard", axis=0, tiled=True)
    fc_cols = exchange(fc_weight, "shard", 1, 0)
    inputs = tokens.astype(jnp.float32)
    normed_f, first_back = jax.vjp(layer_norm, inputs, gain_one, shift_one)
    normed_first = normed_f.astype(low)
    projected = jnp.dot(normed_first, qkv_full, preferred_element_type=jnp.float32)
    query = (projected[:, :D] + q_bias).astype(low)
    keys = projected[:, D : 2 * D].astype(low)
    values = (projected[:, 2 * D :] + v_bias).astype(low)
    attended, logsum = attend_forward(query, keys, values, segments)
    residual = (
        inputs + jnp.dot(attended, proj_full, preferred_element_type=jnp.float32) + proj_bias_full
    )
    cot_f = cotangent.astype(jnp.float32)
    normed_s, second_back = jax.vjp(layer_norm, residual, gain_two, shift_two)
    normed_all = lax.all_gather(normed_s.astype(low), "shard", axis=0, tiled=True)
    cot_later, normed_all = lax.optimization_barrier((cotangent, normed_all))
    cot_all = lax.all_gather(cot_later, "shard", axis=0, tiled=True)
    pre_act = jnp.dot(normed_all, fc_cols, preferred_element_type=jnp.float32) + fc_bias.astype(
        jnp.float32
    )
    activated, gelu_back = jax.vjp(gelu_tanh, pre_act)
    hidden = activated.astype(low)
    grad_hidden = jnp.dot(cot_all, out_weight.T, preferred_element_type=jnp.float32)
    (grad_pre,) = gelu_back(grad_hidden)
    grad_pre_low = grad_pre.astype(low)
    grad_normed_part = jnp.dot(grad_pre_low, fc_cols.T, preferred_element_type=jnp.float32).astype(low)
    grad_normed_low = lax.psum_scatter(grad_normed_part, "shard", scatter_dimension=0, tiled=True)
    term_out_weight = jnp.dot(hidden.T, cot_all, preferred_element_type=jnp.float32) * factor
    term_fc_weight = jnp.dot(normed_all.T, grad_pre_low, preferred_element_type=jnp.float32) * factor
    out_part = jnp.dot(hidden, out_weight, preferred_element_type=jnp.float32).astype(low)
    ff_terms = jnp.concatenate(
        [
            term_out_weight.astype(low).reshape(reps, -1, D),
            by_replica(term_fc_weight.astype(low), shards, reps).reshape(reps, -1, D),
        ],
        axis=1,
    )
    ff_sum = jnp.sum(exchange(ff_terms, "rep", 0, 0).astype(jnp.float32), axis=0).astype(low)
    first_later, attended_later, grad_normed_low, ff_sum = lax.optimization_barrier(
        (normed_first, attended, grad_normed_low, ff_sum)
    )
    first_all = lax.all_gather(first_later, "shard", axis=0, tiled=True)
    grad_normed_second = grad_normed_low.astype(jnp.float32)

    grad_from_norm, second_gain_sum, second_shift_sum = second_back(grad_normed_second)
    grad_residual = cot_f + grad_from_norm
    grad_residual_low = grad_residual.astype(low)
    grad_residual_all = lax.all_gather(grad_residual_low, "shard", axis=0, tiled=True)
    attended_cols = exchange(attended_later, "shard", 1, 0)
    grad_attended = jnp.dot(
        grad_residual_low, proj_full.T, preferred_element_type=jnp.float32
    ).astype(low)
    out_rows = out_weight.shape[0] // reps
    out_piece = ff_sum[:out_rows]
    fc_piece = ff_sum[out_rows:].reshape(D // reps, -1)
    fc_piece = exchange(fc_piece, "shard", 0, 1)
    ff_all = spread(jnp.concatenate([out_piece, fc_piece.reshape(-1, D)]), "rep").astype(jnp.float32)

    grad_query, grad_keys, grad_values = attend_backward(
        query, keys, values, segments, attended, logsum, grad_attended
    )
    grad_projected = jnp.concatenate([grad_query, grad_keys, grad_values], axis=1).astype(low)
    grad_projected, ff_all = lax.optimization_barrier((grad_projected, ff_all))
    out_grad = ff_all[:, :out_rows].reshape(-1, D)
    fc_grad = ff_all[:, out_rows:].reshape(-1, FF)
    grad_cols = exchange(grad_projected, "shard", 1, 0)
    grad_normed_first = jnp.dot(grad_projected, qkv_full.T, preferred_element_type=jnp.float32)
    out_later, grad_cols = lax.optimization_barrier((out_part, grad_cols))
    out_sum = lax.psum_scatter(out_later, "shard", scatter_dimension=0, tiled=True)
    result = (residual + out_sum.astype(jnp.float32) + out_bias_full).astype(low)
    term_qkv_weight = jnp.dot(first_all.T, grad_cols, preferred_element_type=jnp.float32) * factor
    term_proj_weight = (
        jnp.dot(attended_cols.T, grad_residual_all, preferred_element_type=jnp.float32) * factor
    )
    attn_terms = jnp.concatenate(
        [
            term_proj_weight.astype(low).reshape(reps, -1, D),
            by_replica(term_qkv_weight.astype(low), shards, reps).reshape(reps, -1, D),
        ],
        axis=1,
    )
    attn_sum = jnp.sum(exchange(attn_terms, "rep", 0, 0).astype(jnp.float32), axis=0).astype(low)
    proj_rows = proj_weight.shape[0] // reps
    proj_piece = attn_sum[:proj_rows]
    qkv_piece = attn_sum[proj_rows:].reshape(D // reps, -1)
    qkv_piece = exchange(qkv_piece, "shard", 0, 1)
    attn_all = spread(jnp.concatenate([proj_piece, qkv_piece.reshape(-1, D)]), "rep").astype(
        jnp.float32
    )
    proj_grad = attn_all[:, :proj_rows].reshape(-1, D)
    qkv_grad = attn_all[:, proj_rows:].reshape(-1, 3 * D)

    grad_input_norm, first_gain_sum, first_shift_sum = first_back(grad_normed_first)
    grad_inputs = grad_residual + grad_input_norm
    terms = jnp.stack(
        [
            first_gain_sum,
            first_shift_sum,
            jnp.sum(grad_query, axis=0),
            jnp.sum(grad_values, axis=0),
            jnp.sum(grad_residual, axis=0),
            second_gain_sum,
            second_shift_sum,
            jnp.sum(cot_f, axis=0),
        ]
    )
    count = terms.shape[0]
    terms = terms.reshape(count, shards, -1).swapaxes(0, 1).reshape(shards, -1)
    own_terms = jnp.concatenate(
        [jnp.sum(exchange(terms, "shard", 0, 0), axis=0), jnp.sum(grad_pre, axis=0)]
    )
    sums = jnp.sum(spread(own_terms, "rep"), axis=0) * factor
    own_cols = D // shards
    fc_bias_grad = sums[count * own_cols :]
    sums = sums[: count * own_cols].reshape(count, own_cols)
    return (
        result,
        grad_inputs,
        sums[0],
        sums[1],
        qkv_grad,
        sums[2:4],
        proj_grad,
        sums[4],
        sums[5],
        sums[6],
        fc_grad,
        fc_bias_grad,
        out_grad,
        sums[7],
    )


def solution(mesh):
    return jax.shard_map(
        per_device,
        mesh=mesh,
        in_specs=(
            P(("rep", "shard"), None),
            P(("rep", "shard"), None),
            P("shard"),
            P("shard"),
            P("shard", None),
            P(None, "shard"),
            P("shard", None),
            P("shard"),
            P("shard"),
            P("shard"),
            P("shard", None),
            P("shard"),
            P("shard", None),
            P("shard"),
            P(("rep", "shard"), None),
        ),
        out_specs=(
            P(("rep", "shard"), None),
            P(("rep", "shard"), None),
            P("shard"),
            P("shard"),
            P("shard", None),
            P(None, "shard"),
            P("shard", None),
            P("shard"),
            P("shard"),
            P("shard"),
            P("shard", None),
            P("shard"),
            P("shard", None),
            P("shard"),
        ),
        check_vma=False,
    )
```
